32 devices in a mesh: tok: 4 (over x, core), hid: 4 (over z), out: 2 (over y).
Axes of the slice: x: 2, y: 2, z: 4, core: 2. Of those that a mesh axis runs over, the one named last changes fastest.
Arguments:
- tokens: bfloat16 [768, 3072], P('tok', 'hid'), may hold values from -8 to 8
- proj_weight: bfloat16 [3072, 16, 384], P('hid', 'out', 'tok')
- query_gain: float32 [128], replicated, may hold values from 0.6 to 6
- key_gain: float32 [128], replicated, may hold values from 0.6 to 6
- windows: int32 [2, 6], replicated, may hold values from 0 to 1, as said below
- out_weight: bfloat16 [2, 1024, 3072], P('out', 'hid', 'tok'), may hold values from -0.125 to 0.125
Outputs:
- mixed: bfloat16 [768, 3072], P('tok', ('hid', 'out'))
The draws below stay inside these ranges and needn't reach their ends.
Inputs may be any that keep to these rules, and one draw needn't show every extreme that they name: `windows`: entry 2a and 2a + 1 of tile n say whether its window reaches one tile lower and one tile higher along time, height, width (a = 0, 1, 2); where that tile lies outside the grid of 1 x 1 x 2 tiles the entry selects nothing.
All inputs are finite; a program needn't handle non-finite values.
Results may differ from the reference program's by a relative error of at most 0.03.
Values may be sent and summed in bfloat16 or wider, within the bound.
No kernel may reach another device: no remote copies, remote signals or barrier semaphores. Data moves between devices by JAX's collectives and lax.ppermute only.
A program may use at most 64 MiB of HBM per device.

```python
import jax
import jax.numpy as jnp
from jax import lax

D = 3072
HD = 128
H = 16
GH = 1
TILE = 384
TILES = 2
GW = 2
TOKENS = 768
HPO = 8
HPD = 2
N_OUT = 2


def draw_tokens(key, part):
    base_key = jax.random.fold_in(key, 11)
    first = jax.random.fold_in(base_key, 1)
    base = jax.random.normal(first, (TOKENS, D), jnp.float32)
    return jnp.clip(base, -6.0, 6.0).astype(jnp.bfloat16)


def draw_proj_weight(key, part):
    base_key = jax.random.fold_in(key, 23)
    first = jax.random.fold_in(base_key, 1)
    base = jnp.clip(jax.random.normal(first, (D, H, 3 * HD), jnp.float32), -6.0, 6.0) / jnp.sqrt(D * 1.0)
    return base.astype(jnp.bfloat16)


def draw_gain(key, salt):
    inner = jax.random.fold_in(key, salt)
    return jax.random.uniform(inner, (HD,), jnp.float32, 0.6, 1.6)


def draw_query_gain(key, part):
    return draw_gain(key, 31)


def draw_key_gain(key, part):
    return draw_gain(key, 37)


def draw_windows(key, part):
    inner = jax.random.fold_in(key, 41)
    return (jax.random.randint(inner, (TILES, 6), 0, 4) > 0).astype(jnp.int32)


def steps_of(rng, extent, pieces, low, largest):
    factor_of, own = 1.0, jax.random.fold_in(rng, 6)
    for axis_at, parts in pieces:
        steps = jnp.exp(jax.random.uniform(jax.random.fold_in(own, axis_at), (parts,), jnp.float32, low / len(pieces), largest / len(pieces)))
        factor_of = factor_of * jnp.repeat(steps, extent[axis_at] // parts).reshape([-1 if axis == axis_at else 1 for axis in range(len(extent))])
    return factor_of


def centred(own_key, extent, width, most, cuts=(), kind=jnp.bfloat16):
    factor_of = steps_of(own_key, extent, cuts, -0.22, 0.18) if cuts else 1.0
    entries = jax.random.normal(own_key, extent, jnp.float32) * width * factor_of
    return jnp.minimum(jnp.maximum(entries, -most), most).astype(kind)


def setup_inputs(seed: int = 0) -> dict:
    splits = jax.random.split(jax.random.key(seed), 7)
    tokens = draw_tokens(jax.random.fold_in(splits[6], 71), 0)
    proj_weight = draw_proj_weight(jax.random.fold_in(splits[6], 71), 0)
    query_gain = draw_query_gain(jax.random.fold_in(splits[6], 71), 0)
    key_gain = draw_key_gain(jax.random.fold_in(splits[6], 71), 0)
    windows = draw_windows(jax.random.fold_in(splits[6], 71), 0)
    out_weight = centred(splits[5], (N_OUT, HPO * HD, D), (H * HD) ** -0.5, 0.125, ((0, 2), (1, 4), (2, 4)))
    return {"tokens": tokens, "proj_weight": proj_weight, "query_gain": query_gain, "key_gain": key_gain, "windows": windows, "out_weight": out_weight}


def rms_scale(field, gain):
    return field * lax.rsqrt(lax.optimization_barrier(jnp.mean(field * field, axis=-1, keepdims=True)) + 1e-06) * gain

def tile_mask(tile_now, windows, offsets, grid_h, grid_w, tile_count):
    target = tile_now + offsets
    slab = grid_h * grid_w
    d_time = target // slab - tile_now // slab
    d_height = target // grid_w % grid_h - tile_now // grid_w % grid_h
    d_width = target % grid_w - tile_now % grid_w
    limits = lax.dynamic_slice_in_dim(windows, tile_now, 1, 0)[0]
    valid = (target >= 0) & (target < tile_count)
    valid = valid & (d_time >= -limits[0]) & (d_time <= limits[1])
    valid = valid & (d_height >= -limits[2]) & (d_height <= limits[3])
    valid = valid & (d_width >= -limits[4]) & (d_width <= limits[5])
    return valid

def reference(tokens, proj_weight, query_gain, key_gain, windows, out_weight):
    highest_precision = lax.Precision.HIGHEST
    qkv = jnp.einsum('td,dhc->thc', tokens.astype(jnp.float32), proj_weight.astype(jnp.float32), precision=highest_precision)
    query_matrix = rms_scale(qkv[:, :, :HD], query_gain).astype(jnp.bfloat16)
    key_rows = rms_scale(qkv[:, :, HD:2 * HD], key_gain).astype(jnp.bfloat16)
    values = qkv[:, :, 2 * HD:].astype(jnp.bfloat16)
    reach = GH * GW + GW + 1
    query_tiles = query_matrix.reshape(TILES, TILE, H, HD)
    padded_keys = jnp.pad(key_rows.reshape(TILES, TILE, H, HD), ((reach, reach), (0, 0), (0, 0), (0, 0)))
    padded_values = jnp.pad(values.reshape(TILES, TILE, H, HD), ((reach, reach), (0, 0), (0, 0), (0, 0)))
    score_scale = HD ** (-0.5)
    offsets = jnp.arange(2 * reach + 1, dtype=jnp.int32) - reach

    def one_tile(tile_now):
        candidate_key_rows = lax.dynamic_slice_in_dim(padded_keys, tile_now, 2 * reach + 1, 0).reshape(-1, H, HD)
        candidate_value_rows = lax.dynamic_slice_in_dim(padded_values, tile_now, 2 * reach + 1, 0).reshape(-1, H, HD)
        valid = tile_mask(tile_now, windows, offsets, GH, GW, TILES)
        key_ok = jnp.repeat(valid, TILE)
        local_query_rows = lax.dynamic_slice_in_dim(query_tiles, tile_now, 1, 0)[0]
        attention_scores = jnp.einsum('eyw,oyw->yeo', local_query_rows.astype(jnp.float32), candidate_key_rows.astype(jnp.float32), precision=highest_precision) * score_scale
        attention_scores = jnp.where(key_ok[None, None, :], attention_scores, -jnp.inf)
        peak = lax.optimization_barrier(jnp.max(attention_scores, axis=-1, keepdims=True))
        exponent_scores = jnp.exp(attention_scores - peak)
        total = lax.optimization_barrier(jnp.sum(exponent_scores, axis=-1))
        rounded_scores = lax.optimization_barrier(exponent_scores.astype(jnp.bfloat16))
        weighted_value_sum = jnp.einsum('mlz,zme->lme', rounded_scores.astype(jnp.float32), candidate_value_rows.astype(jnp.float32), precision=highest_precision)
        return (weighted_value_sum / jnp.transpose(total)[:, :, None]).astype(jnp.bfloat16)
    attention = lax.map(one_tile, jnp.arange(TILES, dtype=jnp.int32)).reshape(TOKENS, H * HD)
    group_count = H // HPD
    attention_groups = jnp.transpose(attention.reshape(TOKENS, group_count, HPD * HD), (1, 0, 2))
    weight_groups = out_weight.reshape(group_count, HPD * HD, D)

    def add_group(running, pair):
        attention_part, weight_part = pair
        part = jnp.dot(attention_part.astype(jnp.float32), weight_part.astype(jnp.float32), precision=highest_precision)
        rounded_scores = lax.optimization_barrier(part.astype(jnp.bfloat16))
        return (running + rounded_scores.astype(jnp.float32), None)
    weighted_value_sum, unused = lax.scan(add_group, jnp.zeros((TOKENS, D), jnp.float32), (attention_groups, weight_groups))
    return weighted_value_sum.astype(jnp.bfloat16)
```

```python
import functools

import jax
import jax.numpy as jnp
from jax import lax
from jax.experimental import pallas as pl
from jax.experimental.pallas import tpu as pltpu
from jax.sharding import PartitionSpec as P

HD = 128
GH = 1


def from_partner(value, axis, bit):
    mask = 2**bit
    pairs = [(source, source ^ mask) for source in range(lax.axis_size(axis))]
    return lax.ppermute(value, axis, pairs)


def swap(value, axis, mask):
    pairs = [(source, source ^ mask) for source in range(lax.axis_size(axis))]
    return lax.ppermute(value, axis, pairs)


def from_behind(shard, axis, by):
    length = lax.axis_size(axis)
    pairs = [(i, i + by) for i in range(length) if 0 <= i + by < length]
    return lax.ppermute(shard, axis, pairs)


def rms_scale(field, gain):
    return field * lax.rsqrt(jnp.mean(field * field, axis=-1, keepdims=True) + 1e-06) * gain


def tile_mask(tile_now, windows, offsets, grid_h, grid_w, tile_count):
    target = tile_now + offsets
    slab = grid_h * grid_w
    d_time = target // slab - tile_now // slab
    d_height = target // grid_w % grid_h - tile_now // grid_w % grid_h
    d_width = target % grid_w - tile_now % grid_w
    limits = lax.dynamic_slice_in_dim(windows, tile_now, 1, 0)[0]
    valid = (target >= 0) & (target < tile_count)
    valid = valid & (d_time >= -limits[0]) & (d_time <= limits[1])
    valid = valid & (d_height >= -limits[2]) & (d_height <= limits[3])
    valid = valid & (d_width >= -limits[4]) & (d_width <= limits[5])
    return valid


def gathered_weights_body(tokens, proj_weight, query_gain, key_gain, windows, out_weight):
    device_count = lax.axis_size("tok")
    tile_count = device_count // 2
    grid_w = min(8, device_count // 2)
    grid_h = GH
    slab = grid_h * grid_w
    row_count = tokens.shape[0]
    partial_value = jnp.einsum(
        "rd,dhc->rhc",
        tokens,
        lax.all_gather(proj_weight, "tok", axis=2, tiled=True),
        preferred_element_type=jnp.float32,
    )
    qkv = lax.psum_scatter(
        partial_value.astype(jnp.bfloat16), "hid", scatter_dimension=1, tiled=True
    ).astype(jnp.float32)
    head_count = qkv.shape[1]
    width = head_count * HD
    query_matrix = rms_scale(qkv[:, :, :HD], query_gain).astype(jnp.bfloat16)
    key_rows = rms_scale(qkv[:, :, HD : 2 * HD], key_gain).astype(jnp.bfloat16)
    values = qkv[:, :, 2 * HD :].astype(jnp.bfloat16)
    half_pair = jnp.concatenate(
        [key_rows.reshape(row_count, width), values.reshape(row_count, width)], axis=1
    )
    partner = from_partner(half_pair, "tok", 0)
    place = lax.axis_index("tok")
    parity = place % 2
    tile_now = place // 2
    whole = jnp.where(
        parity == 0,
        jnp.concatenate([half_pair, partner], axis=0),
        jnp.concatenate([partner, half_pair], axis=0),
    )
    offset_list = sorted(
        set(
            (
                d_t * slab + d_h * grid_w + d_w
                for d_t in (-1, 0, 1)
                for d_h in (-1, 0, 1)
                for d_w in (-1, 0, 1)
            )
        )
    )
    pieces = []
    for offset in offset_list:
        if offset == 0:
            pieces.append(whole)
        else:
            pieces.append(from_behind(whole, "tok", -2 * offset))
    candidates = jnp.stack(pieces, axis=0)
    offsets = jnp.array(offset_list, dtype=jnp.int32)
    valid = tile_mask(tile_now, windows, offsets, grid_h, grid_w, tile_count)
    key_ok = jnp.repeat(valid, whole.shape[0])
    flat = candidates.reshape(-1, 2 * width)
    candidate_key_rows = flat[:, :width].reshape(-1, head_count, HD)
    candidate_value_rows = flat[:, width:].reshape(-1, head_count, HD)
    score_scale = HD ** (-0.5)
    attention_scores = (
        jnp.einsum(
            "eyw,oyw->yeo", query_matrix, candidate_key_rows, preferred_element_type=jnp.float32
        )
        * score_scale
    )
    attention_scores = jnp.where(key_ok[None, None, :], attention_scores, -jnp.inf)
    peak = jnp.max(attention_scores, axis=-1, keepdims=True)
    exponent_scores = jnp.exp(attention_scores - peak)
    total = jnp.sum(exponent_scores, axis=-1)
    weighted_value_sum = jnp.einsum(
        "mlz,zme->lme",
        exponent_scores.astype(jnp.bfloat16),
        candidate_value_rows,
        preferred_element_type=jnp.float32,
    )
    attention = (
        (weighted_value_sum / jnp.transpose(total)[:, :, None])
        .astype(jnp.bfloat16)
        .reshape(row_count, width)
    )
    out_part = jnp.dot(
        attention,
        lax.all_gather(out_weight, "tok", axis=2, tiled=True)[0],
        preferred_element_type=jnp.float32,
    )
    return lax.psum_scatter(
        out_part.astype(jnp.bfloat16), ("hid", "out"), scatter_dimension=1, tiled=True
    )


VMEM = pltpu.VMEM
SMEM = pltpu.SMEM


def spec(space):
    return pl.BlockSpec(memory_space=space)


def kernel_call(body, outs, inputs, scratch=(), flops=0, smem=(), name=None):
    specs = [spec(SMEM if i in smem else VMEM) for i in range(len(inputs))]
    moved = sum(x.size * x.dtype.itemsize for x in (*inputs, *outs))
    return pl.pallas_call(
        body,
        out_shape=tuple(outs),
        in_specs=specs,
        out_specs=tuple(spec(VMEM) for _ in outs),
        scratch_shapes=list(scratch),
        cost_estimate=pl.CostEstimate(flops=flops, bytes_accessed=moved, transcendentals=0),
        name=name,
    )(*inputs)


def project_kernel(count, w_ref, first_ref, second_ref, *rest):
    outs, rows = rest[:count], rest[count]
    half = first_ref.shape[0]
    rows[:half] = first_ref[...]
    rows[half:] = second_ref[...]
    place = lax.axis_index("hid")
    for mask in range(count):
        product = lax.dot_general(
            w_ref[place ^ mask],
            rows[...],
            (((1,), (1,)), ((), ())),
            preferred_element_type=jnp.float32,
        )
        outs[mask][...] = product.astype(outs[mask].dtype)


def project(weight, first, second, count):
    _, width, depth = weight.shape
    n = first.shape[0] + second.shape[0]
    out = jax.ShapeDtypeStruct((width, n), jnp.bfloat16)
    return kernel_call(
        functools.partial(project_kernel, count),
        [out] * count,
        [weight, first, second],
        scratch=[VMEM((n, depth), first.dtype)],
        flops=2 * count * width * depth * n,
        name="project",
    )


def sum_kernel(*refs):
    ins, out = refs[:-1], refs[-1]
    total = ins[0][...].astype(jnp.float32)
    for ref in ins[1:]:
        total += ref[...].astype(jnp.float32)
    out[...] = total.astype(out.dtype)


def add_up(parts, name):
    out = jax.ShapeDtypeStruct(parts[0].shape, jnp.bfloat16)
    return kernel_call(sum_kernel, [out], parts, flops=len(parts) * out.size, name=name)[0]


def order_kernel(*refs):
    blocks, out = refs[:-1], refs[-1]
    base = lax.axis_index("hid") ^ lax.axis_index("tok")
    for r, ref in enumerate(blocks):
        out[base ^ r] = ref[...]


def attention_kernel(
    tile_of, heads, win_ref, qg_ref, kg_ref, *refs
):
    ins, out, cols = refs[:8], refs[8], refs[9]
    place = lax.axis_index("tok")
    half = ins[0].shape[1]
    quarter = half // 2
    width = ins[0].shape[0] // heads
    for r in range(4):
        pair = (ins[2 * r], ins[2 * r + 1])
        if r & 2:
            pair = pair[::-1]
        for j, ref in enumerate(pair):
            block = ref[...]
            if r & 1:
                block = jnp.concatenate([block[:, quarter:], block[:, :quarter]], axis=1)
            for h in range(heads):
                cols[place ^ r, h, :, j * half : (j + 1) * half] = block[
                    h * width : (h + 1) * width
                ]
    tile_now, other, grid_h, grid_w = tile_of(place)
    slab = grid_h * grid_w
    moves = (
        other // slab - tile_now // slab,
        (other // grid_w) % grid_h - (tile_now // grid_w) % grid_h,
        other % grid_w - tile_now % grid_w,
    )
    valid = None
    for axis, move in enumerate(moves):
        fits = (move >= -win_ref[tile_now, 2 * axis]) & (move <= win_ref[tile_now, 2 * axis + 1])
        valid = fits if valid is None else valid & fits
    bias = jnp.where(valid, 0.0, -jnp.inf)
    scale = HD ** (-0.5)

    def rms(u, gain):
        mean = jnp.mean(u * u, axis=0, keepdims=True)
        return (u * lax.rsqrt(mean + 1e-06) * gain).astype(jnp.bfloat16)

    for h in range(heads):
        full = cols[:, h].reshape(4 * width, 2 * half)
        query = rms(full[:HD, :quarter].astype(jnp.float32), qg_ref[...])
        key = rms(full[HD : 2 * HD].astype(jnp.float32), kg_ref[...])
        scores = lax.dot_general(
            key, query, (((0,), (0,)), ((), ())), preferred_element_type=jnp.float32
        )
        scores = scores * scale
        near, far = scores[:half], scores[half:] + bias
        peak = jnp.maximum(
            jnp.max(near, axis=0, keepdims=True), jnp.max(far, axis=0, keepdims=True)
        )
        near, far = jnp.exp(near - peak), jnp.exp(far - peak)
        total = jnp.sum(near, axis=0, keepdims=True) + jnp.sum(far, axis=0, keepdims=True)
        weights = jnp.concatenate([near, far], axis=0).astype(jnp.bfloat16)
        mixed = jnp.dot(full[2 * HD :], weights, preferred_element_type=jnp.float32)
        out[:, h * HD : (h + 1) * HD] = jnp.transpose(mixed / total).astype(out.dtype)


def output_kernel(count, own_ref, other_ref, w_ref, *outs):
    width = own_ref.shape[1]
    for mask in range(count):
        product = jnp.dot(
            own_ref[...], w_ref[mask, :width], preferred_element_type=jnp.float32
        ) + jnp.dot(other_ref[...], w_ref[mask, width:], preferred_element_type=jnp.float32)
        outs[mask][...] = product.astype(outs[mask].dtype)


def moved_tokens_body(tokens, proj_weight, query_gain, key_gain, windows, out_weight):
    tok, hid, sides = (lax.axis_size(a) for a in ("tok", "hid", "out"))
    rows, depth = tokens.shape
    _, heads_here, width = proj_weight.shape
    heads = heads_here // hid
    weight = jnp.transpose(proj_weight, (1, 2, 0)).reshape(hid, heads * width, depth)

    tokens_core = swap(tokens, "tok", 1)
    tokens_chip = swap(tokens, "tok", 2)
    near = project(weight, tokens, tokens_core, hid)
    near_got = [swap(near[m], "hid", m) for m in range(1, hid)]
    tokens_diag = swap(tokens_chip, "tok", 1)
    far = project(weight, tokens_chip, tokens_diag, hid)
    far_got = [swap(far[m], "hid", m) for m in range(1, hid)]

    side = lax.axis_index("out")
    piece = out_weight.shape[2] // sides
    split = out_weight[0].reshape(out_weight.shape[1], sides, piece)
    mine = lax.dynamic_index_in_dim(split, side, 1, keepdims=False)
    theirs = lax.dynamic_index_in_dim(split, side ^ 1, 1, keepdims=False)
    got = swap(theirs, "out", 1)
    block = jnp.concatenate([mine, got], axis=0)
    block_chip = swap(block, "tok", 2)
    block_core = swap(block, "tok", 1)
    block_diag = swap(block_chip, "tok", 1)
    ordered = kernel_call(
        order_kernel,
        [jax.ShapeDtypeStruct((hid, *block.shape), block.dtype)],
        [block, block_core, block_chip, block_diag],
        name="order",
    )[0]

    near_sum = add_up([near[0], *near_got], "add_near")
    near_chip = swap(near_sum, "tok", 2)
    near_core = swap(near_sum, "tok", 1)
    near_diag = swap(near_chip, "tok", 1)
    far_sum = add_up([far[0], *far_got], "add_far")
    far_chip = swap(far_sum, "tok", 2)
    far_core = swap(far_sum, "tok", 1)
    far_diag = swap(far_chip, "tok", 1)

    grid_w = min(8, tok // 2)

    def tile_of(place):
        tile = place // 2
        return tile, tile ^ 1, GH, grid_w

    n = rows * tok
    attention = kernel_call(
        functools.partial(attention_kernel, tile_of, heads),
        [jax.ShapeDtypeStruct((rows, heads * HD), jnp.bfloat16)],
        [
            windows,
            query_gain.reshape(HD, 1),
            key_gain.reshape(HD, 1),
            near_sum,
            far_sum,
            near_core,
            far_core,
            near_chip,
            far_chip,
            near_diag,
            far_diag,
        ],
        scratch=[VMEM((tok, heads, width, n), jnp.bfloat16)],
        flops=4 * heads * rows * n * HD,
        smem=(0,),
        name="attention",
    )[0]
    attention_side = swap(attention, "out", 1)
    parts = kernel_call(
        functools.partial(output_kernel, hid),
        [jax.ShapeDtypeStruct((rows, piece), jnp.bfloat16)] * hid,
        [attention, attention_side, ordered],
        flops=2 * rows * ordered.size,
        name="output",
    )
    parts_got = [swap(parts[m], "hid", m) for m in range(1, hid)]
    return add_up([parts[0], *parts_got], "add_out")


def solution(mesh):
    in_specs = (P("tok", "hid"), P("hid", "out", "tok"), P(), P(), P(), P("out", "hid", "tok"))
    out_specs = P("tok", ("hid", "out"))
    tok, hid, sides = (mesh.shape[a] for a in ("tok", "hid", "out"))
    small = tok // 2 == 2 and hid == tok and sides == 2
    body = moved_tokens_body if small else gathered_weights_body
    return jax.shard_map(body, mesh=mesh, in_specs=in_specs, out_specs=out_specs, check_vma=False)
```
